32 devices in a mesh: px: 2 (over y), py: 4 (over z), case: 4 (over x, core).
Axes of the slice: x: 2, y: 2, z: 4, core: 2. Of those that a mesh axis runs over, the one named last changes fastest.
Arguments:
- comp_type: int32 [1024], P(('px', 'py')), may hold values from 0 to 7
- stiffness: float32 [1024], P(('px', 'py')), may hold values from 0.3 to 3
- near_port: int32 [1024], P(('px', 'py')), may hold values from 0 to 127
- far_owner: int32 [1024, 1], P(('px', 'py')), may hold values from 0 to 7; in each aligned block of 128 rows (0 to 127, 128 to 255, ...) at most 24 rows name the same one
- far_port: int32 [1024], P(('px', 'py')), may hold values from 0 to 127
- bubble_load: float32 [64, 32, 1024], P(None, 'case', ('px', 'py')), may hold values from -6 to 6
- port_load: float32 [48, 32, 1024], P(None, 'case', ('px', 'py')), may hold values from -3 to 3
- bubble_inverse: float32 [8, 64, 64], replicated, may hold values from -1.5 to 2, as said below
- coupling: float32 [8, 96, 64], replicated, may hold values from -0.1 to 0.1
- port_block: float32 [8, 96, 96], replicated, may hold values from -3 to 8, as said below
Outputs:
- port_solution: float32 [48, 32, 1024], P(None, 'case', ('px', 'py'))
- port_residual: float32 [48, 32, 1024], P(None, 'case', ('px', 'py'))
- bubble_solution: float32 [64, 32, 1024], P(None, 'case', ('px', 'py'))
The draws below stay inside these ranges and needn't reach their ends.
Inputs may be any that keep to these rules, and one draw needn't show every extreme that they name: `far_owner`: among the 128 components of one partition, at most 24 name the same owner, a bound that some block reaches. `bubble_inverse`: each matrix is symmetric positive definite. `port_block`: each matrix is symmetric positive definite.
All inputs are finite; a program needn't handle non-finite values.
Results may differ from the reference program's by a relative error of at most 0.00016.
Values sent between devices are 32-bit elements; how exact they have to be, the bound alone decides.
A program may use at most 64 MiB of HBM per device.

```python
import math
import jax
import jax.numpy as jnp
import numpy as np
from jax import lax

MODES = 64
PD = 48
TYPES = 8
ITERS = 2
COMP_DEV = 128
NPART = 8
PORT_DEV = 128
CAP = 24
COMPONENTS = 1024
PORTS = 1024
CASES = 32
N_PX = 2
N_PY = 4


def draw_bubble_inverse(key, part):
    base = jax.random.uniform(key, (TYPES, MODES, MODES), jnp.float32, -1.7, 1.7)
    square = jnp.einsum('tij,tkj->tik', base, base) / MODES
    return 0.5 * jnp.eye(MODES, dtype=jnp.float32)[None, :, :] + 0.5 * square


def draw_port_block(key, part):
    size_ports = 2 * PD
    base = jax.random.uniform(key, (TYPES, size_ports, size_ports), jnp.float32, -1.7, 1.7)
    square = jnp.einsum('tij,tkj->tik', base, base) / size_ports
    return 5.0 * jnp.eye(size_ports, dtype=jnp.float32)[None, :, :] + square


def place_ends(array, stream_key, low, largest):
    spot = [jax.random.randint(jax.random.fold_in(stream_key, axis), (), 0, length) for axis, length in enumerate(array.shape)]
    widest = array.shape.index(max(array.shape))
    neighbour = spot[:widest] + [(spot[widest] + 1) % array.shape[widest]] + spot[widest + 1:]
    return array.at[tuple(spot)].set(low).at[tuple(neighbour)].set(largest)


def shard_levels(rng, extent, pieces, least, largest):
    loudness, own = 1.0, jax.random.fold_in(rng, 6)
    for position, parts in pieces:
        draws = jnp.exp(jax.random.uniform(jax.random.fold_in(own, position), (parts,), jnp.float32, least / len(pieces), largest / len(pieces)))
        loudness = loudness * jnp.repeat(draws, extent[position] // parts).reshape([-1 if axis == position else 1 for axis in range(len(extent))])
    return loudness


def assign_block(rng, own, number, rows, count, top, most, lean):
    sequence = jax.random.permutation(rng, count)
    crowded, common = shares(count, rows * top, most, lean, True), shares(count, rows * top, most, lean, False)
    places = jnp.arange(count)

    def named(sizes, rotation):
        used = int((sizes > 0).sum())
        fixed = max(1, used // 4)
        moved = fixed + (places - fixed + rotation * (used - fixed)) % max(1, count - fixed)
        return jnp.zeros((count,), jnp.int32).at[sequence[jnp.where(places < fixed, places, moved)]].set(jnp.asarray(sizes, jnp.int32))

    sizes = jnp.where(number % 4 == 0, named(crowded, number // 4), named(common, number - number // 4 - 1))
    mixed = jax.random.permutation(jax.random.fold_in(own, 3), count)
    source_of, taker = mixed[0:count // 2 * 2:2], mixed[1:count // 2 * 2:2]
    slack = jnp.minimum(sizes[source_of] - 1, most - sizes[taker]) // 2
    slack = jnp.where((source_of == sequence[0]) | (taker == sequence[0]) | (sizes[taker] == 0), 0, jnp.maximum(slack, 0))
    moved = jax.random.randint(jax.random.fold_in(own, 4), (count // 2,), 0, 1 << 20) % (slack + 1)
    sizes = sizes.at[source_of].add(-moved).at[taker].add(moved)
    labels = jnp.searchsorted(jnp.cumsum(sizes), jnp.arange(rows * top), side="right").astype(jnp.int32)
    table = labels.reshape(top, rows).T
    table = table[jax.random.permutation(jax.random.fold_in(own, 1), rows)]
    rotation = jax.random.randint(jax.random.fold_in(own, 2), (rows, 1), 0, top)
    return jnp.take_along_axis(table, (jnp.arange(top)[None, :] + rotation) % top, axis=1)


def shares(number_of, total, reach, skew, full):
    weights = [(1 << 20) // math.isqrt(standing ** skew) + 1 for standing in range(1, number_of + 1)]
    largest = reach if full else min(reach, max(-(-total // number_of), total * weights[0] // sum(weights)))
    least = 1 if total - largest >= number_of - 1 else 0
    counts, surplus = [largest] + [least] * (number_of - 1), total - largest - least * (number_of - 1)
    while surplus > 0:
        free = [i for i in range(1, number_of) if counts[i] < largest] or [i for i in range(1, number_of) if counts[i] < reach]
        pool, remaining = sum([weights[i] for i in free]), surplus
        for i in free:
            extra = min(reach - counts[i], max(1, remaining * weights[i] // pool), surplus)
            counts[i] = counts[i] + extra
            surplus = surplus - extra
    return np.array(counts)


def normal_values(key, dims, spread, most, pieces=(), kind=jnp.bfloat16):
    values = spread * jax.random.normal(key, dims, jnp.float32)
    if pieces:
        values = values * shard_levels(key, dims, pieces, -0.22, 0.18)
    return jnp.clip(values, -most, most).astype(kind)


def setup_inputs(seed: int = 0) -> dict:
    key_of = jax.random.split(jax.random.key(seed), 11)
    comp_type = place_ends(jax.random.randint(key_of[0], (COMPONENTS,), 0, TYPES), jax.random.fold_in(key_of[0], 1), 0, TYPES - 1).astype(jnp.int32)
    stiffness = jnp.clip(jnp.exp(math.log(3.0) - 2.3025851 * jax.random.uniform(key_of[1], (COMPONENTS,), jnp.float32) ** shard_levels(key_of[1], (COMPONENTS,), ((0, 8),), -0.2, 0.2)), 0.3, 3.0)
    near_port = place_ends(jax.random.randint(key_of[2], (COMPONENTS,), 0, PORT_DEV), jax.random.fold_in(key_of[2], 1), 0, PORT_DEV - 1).astype(jnp.int32)
    far_owner_keys = jax.random.split(jax.random.fold_in(key_of[3], 1), COMPONENTS // COMP_DEV)
    far_owner_turns = jax.random.permutation(jax.random.fold_in(key_of[3], 3), COMPONENTS // COMP_DEV)
    far_owner = jax.vmap(lambda own, number: assign_block(jax.random.fold_in(key_of[3], 2), own, number, COMP_DEV, NPART, 1, CAP, 2))(far_owner_keys, far_owner_turns).reshape((COMPONENTS, 1))
    far_port = place_ends(jax.random.randint(key_of[4], (COMPONENTS,), 0, PORT_DEV), jax.random.fold_in(key_of[4], 1), 0, PORT_DEV - 1).astype(jnp.int32)
    bubble_load = normal_values(key_of[5], (MODES, CASES, COMPONENTS), 1.0, 6.0, ((1, 4), (2, 8)), jnp.float32)
    port_load = normal_values(key_of[6], (PD, CASES, PORTS), 0.5, 3.0, ((1, 4), (2, 8)), jnp.float32)
    bubble_inverse = draw_bubble_inverse(jax.random.fold_in(key_of[10], 71), 0)
    coupling = jnp.clip(jax.random.uniform(key_of[8], (TYPES, 2 * PD, MODES), jnp.float32, -0.1, 0.1), -0.1, 0.1)
    port_block = draw_port_block(jax.random.fold_in(key_of[10], 71), 0)
    return {"comp_type": comp_type, "stiffness": stiffness, "near_port": near_port, "far_owner": far_owner, "far_port": far_port, "bubble_load": bubble_load, "port_load": port_load, "bubble_inverse": bubble_inverse, "coupling": coupling, "port_block": port_block}


HIGH = lax.Precision.HIGHEST

def type_tables(bubble_inverse, coupling, port_block):
    reduced = jnp.einsum('tpm,tmn->tpn', coupling, bubble_inverse, precision=HIGH)
    schur_table = port_block - jnp.einsum('tpm,tqm->tpq', reduced, coupling, precision=HIGH)
    return (reduced, schur_table)

def apply_tables(table, comp_type, factor, vectors):
    in_rows = vectors.shape[0]
    case_count = vectors.shape[1]
    part_count = N_PX * N_PY
    vector_blocks = vectors.reshape(in_rows, case_count, part_count, COMP_DEV).transpose(2, 0, 1, 3)
    kind_blocks = comp_type.reshape(part_count, COMP_DEV)
    factor_blocks = factor.reshape(part_count, COMP_DEV)

    def one_block(packed):
        vector_part, kind_part, factor_part = packed
        matrices = jnp.take(table, kind_part, axis=0)
        result = jnp.einsum('cyx,xkc->ykc', matrices, vector_part, precision=HIGH)
        return result * factor_part[None, None, :]
    results = lax.map(one_block, (vector_blocks, kind_blocks, factor_blocks))
    return results.transpose(1, 2, 0, 3).reshape(results.shape[1], case_count, part_count * COMP_DEV)

def port_indices(near_port, far_owner, far_port):
    owners = jnp.arange(COMPONENTS, dtype=jnp.int32) // COMP_DEV
    return (owners * PORT_DEV + near_port, far_owner[:, 0] * PORT_DEV + far_port)

def spread_ports(port_field, near_global, far_global):
    return jnp.concatenate([jnp.take(port_field, near_global, axis=2), jnp.take(port_field, far_global, axis=2)], axis=0)

def assemble(values, near_global, far_global):
    near_sum = jax.ops.segment_sum(jnp.moveaxis(values[:PD], 2, 0), near_global, num_segments=PORTS)
    far_sum = jax.ops.segment_sum(jnp.moveaxis(values[PD:], 2, 0), far_global, num_segments=PORTS)
    return jnp.moveaxis(near_sum + far_sum, 0, 2)

def port_gram(lhs_field, rhs_field):
    product = jnp.einsum('dkp,djp->kj', lhs_field, rhs_field, precision=HIGH)
    return 0.5 * (product + product.T)

def combine_columns(port_field, weights):
    return jnp.einsum('djp,jk->dkp', port_field, weights, precision=HIGH)

def spd_solve(matrix, target):
    factor = jnp.linalg.cholesky(matrix)
    middle = lax.linalg.triangular_solve(factor, target, left_side=True, lower=True)
    return lax.linalg.triangular_solve(factor, middle, left_side=True, lower=True, transpose_a=True)

def reference(comp_type, stiffness, near_port, far_owner, far_port, bubble_load, port_load, bubble_inverse, coupling, port_block):
    reduced, schur_table = type_tables(bubble_inverse, coupling, port_block)
    near_global, far_global = port_indices(near_port, far_owner, far_port)
    unit_scale = jnp.ones_like(stiffness)
    condensed = -apply_tables(reduced, comp_type, unit_scale, bubble_load)
    rhs_field = port_load + assemble(condensed, near_global, far_global)

    def operate(port_field):
        local_field = spread_ports(port_field, near_global, far_global)
        return assemble(apply_tables(schur_table, comp_type, stiffness, local_field), near_global, far_global)
    solution = jnp.zeros_like(rhs_field)
    residual = rhs_field
    direction = rhs_field
    residual_gram = port_gram(residual, residual)
    for iteration in range(ITERS):
        image_field = operate(direction)
        curvature = port_gram(direction, image_field)
        step_coef = spd_solve(curvature, residual_gram)
        solution = solution + combine_columns(direction, step_coef)
        residual = residual - combine_columns(image_field, step_coef)
        if iteration + 1 < ITERS:
            next_gram = port_gram(residual, residual)
            update_coef = spd_solve(residual_gram, next_gram)
            direction = residual + combine_columns(direction, update_coef)
            residual_gram = next_gram
    port_values = spread_ports(solution, near_global, far_global)
    transposed = jnp.transpose(reduced, (0, 2, 1))
    bubble_solution = apply_tables(bubble_inverse, comp_type, 1.0 / stiffness, bubble_load) - apply_tables(transposed, comp_type, unit_scale, port_values)
    return (solution, residual, bubble_solution)
```

```python
import jax
import jax.numpy as jnp
from jax import lax
from jax.experimental import pallas as pl
from jax.experimental.pallas import tpu as pltpu
from jax.sharding import PartitionSpec as P

HIGH = lax.Precision.HIGHEST
F32 = jnp.float32
BF16 = jnp.bfloat16
MESH = pl.DeviceIdType.MESH
NT = (((1,), (1,)), ((), ()))
TN = (((0,), (0,)), ((), ()))


def split(x):
    top = x.astype(BF16)
    return top, (x - top.astype(F32)).astype(BF16)


def mm(a, b):
    return jnp.dot(a, b, preferred_element_type=F32)


def exact(a, b, dims=(((1,), (0,)), ((), ()))):
    return lax.dot_general(a, b, dims, precision=HIGH, preferred_element_type=F32)


def gauss_solve(matrix, target):
    n = matrix.shape[0]
    aug = jnp.concatenate([matrix, target], axis=1)
    rows = lax.broadcasted_iota(jnp.int32, aug.shape, 0)
    for j in range(n):
        row = aug[j:j + 1, :]
        row = row / row[:, j:j + 1]
        aug = jnp.where(rows == j, row, aug - aug[:, j:j + 1] * row)
    return aug[:, n:]


def kernel(
    sizes,
    idx_ref,
    stiff_ref,
    bload_ref,
    pload_ref,
    binv_ref,
    coup_ref,
    pblock_ref,
    sol_ref,
    res_ref,
    bub_ref,
    ask_send,
    ask_recv,
    far_send,
    far_recv,
    nat,
    gath,
    rows_all,
    gram_send,
    gram_recv,
    inv_keep,
    part_ssem,
    part_rsem,
    case_ssem,
    case_rsem,
):
    parts, npy, nq, depth = sizes
    kinds = binv_ref.shape[0]
    modes, ncase, ncomp = bload_ref.shape
    pd = pload_ref.shape[0]
    nport = pload_ref.shape[2]
    slots = parts * depth
    allcase = nq * ncase
    my_x, my_y, my_c = lax.axis_index("px"), lax.axis_index("py"), lax.axis_index("case")
    me = my_x * npy + my_y

    def part_id(step):
        other = lax.rem(me + step + parts, parts)
        return (other // npy, lax.rem(other, npy), my_c)

    def case_id(step):
        return (my_x, my_y, lax.rem(my_c + step, nq))

    barrier = pltpu.get_barrier_semaphore()

    def greet_part(i, _):
        pl.semaphore_signal(barrier, inc=1, device_id=part_id(i), device_id_type=MESH)
        return 0

    lax.fori_loop(1, parts, greet_part, 0)
    for i in range(1, nq):
        pl.semaphore_signal(barrier, inc=1, device_id=case_id(i), device_id_type=MESH)

    kind_row = idx_ref[0:1, :]
    near_row = idx_ref[1:2, :]
    owner_row = idx_ref[2:3, :]
    far_row = idx_ref[3:4, :]

    def as_column(row):
        return jnp.broadcast_to(row.astype(F32), (ncomp, ncomp)).T

    sub = lax.broadcasted_iota(jnp.int32, (ncomp, ncomp), 0)
    lane = lax.broadcasted_iota(jnp.int32, (ncomp, ncomp), 1)
    same = (as_column(owner_row) == owner_row.astype(F32)) & (sub < lane)
    rank = jnp.sum(jnp.where(same, 1.0, 0.0), axis=0, keepdims=True).astype(jnp.int32)
    slot_row = lax.rem(owner_row - me + parts, parts) * depth + rank
    slot_sub = lax.broadcasted_iota(jnp.int32, (slots, ncomp), 0)
    slot_f = jnp.where(slot_sub == slot_row, 1.0, 0.0)
    slot_pick = slot_f.astype(BF16)
    wanted = jnp.sum(slot_f * (far_row + 1).astype(F32), axis=1, keepdims=True) - 1.0
    wanted = jnp.broadcast_to(wanted, (slots, nport)).reshape(parts, depth, nport)
    ask_send[...] = wanted
    ask_recv[0] = wanted[0]
    near_in = jnp.where(sub == near_row, 1.0, 0.0).astype(BF16)
    near_out = jnp.where(lane.astype(F32) == as_column(near_row), 1.0, 0.0).astype(BF16)

    pl.semaphore_wait(barrier, parts - 1 + nq - 1)

    def send_parts(src, dst, e, sign):
        def body(i, _):
            pltpu.make_async_remote_copy(
                src_ref=src(i),
                dst_ref=dst(i),
                send_sem=part_ssem.at[e],
                recv_sem=part_rsem.at[e],
                device_id=part_id(i if sign > 0 else -i),
                device_id_type=MESH,
            ).start()
            return 0

        if parts <= 8:
            for i in range(1, parts):
                body(i, 0)
        else:
            lax.fori_loop(1, parts, body, 0)

    def wait_on(ref, sem):
        pltpu.make_async_copy(ref, ref, sem).wait()

    rest = pl.ds(1, parts - 1)
    send_parts(lambda i: ask_send.at[i], lambda i: ask_recv.at[i], 6, 1)

    red = [exact(coup_ref[t], binv_ref[t]) for t in range(kinds)]
    schur = [pblock_ref[t] - exact(red[t], coup_ref[t], NT) for t in range(kinds)]
    inv_tab = split(jnp.concatenate([binv_ref[t] for t in range(kinds)], axis=1))
    coup_tab = split(jnp.concatenate([coup_ref[t] for t in range(kinds)], axis=1))
    schur_tab = split(jnp.concatenate(schur, axis=1))
    red_tab = split(jnp.concatenate([r.T for r in red], axis=1))

    def tile_cases(row):
        return jnp.concatenate([row] * ncase, axis=1)

    stiff = tile_cases(stiff_ref[...])
    kind_all = tile_cases(kind_row)
    masks = [jnp.where(kind_all == t, 1.0, 0.0).astype(BF16) for t in range(kinds)]

    def apply_tables(tab, x):
        top, low = split(x)
        xt = jnp.concatenate([top * m for m in masks], axis=0)
        xl = jnp.concatenate([low * m for m in masks], axis=0)
        return mm(tab[0], xt) + mm(tab[0], xl) + mm(tab[1], xt)

    def wide(field, rows):
        return jnp.concatenate(
            [field[k * rows:(k + 1) * rows] for k in range(ncase)], axis=1
        )

    def tall(x):
        return jnp.concatenate(
            [x[:, k * ncomp:(k + 1) * ncomp] for k in range(ncase)], axis=0
        )

    def pick(x, onehot):
        top, low = split(x)
        return mm(jnp.concatenate([top, low], axis=1), jnp.concatenate([onehot, onehot], axis=0))

    def start_far(e, onehot, x, sign):
        top, low = split(x)
        out = lax.dot_general(
            jnp.concatenate([onehot, onehot], axis=1),
            jnp.concatenate([top, low], axis=1),
            NT,
            preferred_element_type=F32,
        ).reshape(parts, depth, x.shape[0])
        far_send[e] = out
        far_recv[e, 0] = out[0]
        send_parts(lambda i: far_send.at[e, i], lambda i: far_recv.at[e, i], e, sign)

    def finish_far(e, onehot):
        wait_on(far_recv.at[e, rest], part_rsem.at[e])
        got = far_recv[e].reshape(slots, ncase * pd).T
        top, low = split(got)
        return mm(top, onehot) + mm(low, onehot)

    def publish(f, field):
        for k in range(ncase):
            nat[f, :, k, :] = field[k * pd:(k + 1) * pd]
        for i in range(1, nq):
            pltpu.make_async_remote_copy(
                src_ref=nat.at[f],
                dst_ref=gath.at[f, i],
                send_sem=case_ssem.at[f],
                recv_sem=case_rsem.at[f],
                device_id=case_id(i),
                device_id_type=MESH,
            ).start()

    def collect(f):
        wait_on(gath.at[f, pl.ds(1, nq - 1)], case_rsem.at[f])

        def body(d, _):
            cols = pl.ds(pl.multiple_of(d * nport, nport), nport)
            rows_all[pl.ds(f * allcase, ncase), cols] = nat[f, d]
            for q in range(1, nq):
                rows_all[pl.ds(f * allcase + q * ncase, ncase), cols] = gath[f, q, d]
            return 0

        lax.fori_loop(0, pd, body, 0)

    def start_gram(s, value):
        h, w = value.shape
        gram_send[s] = jnp.zeros(gram_send.shape[1:], F32)
        gram_send[s, 0:h, 0:w] = value
        gram_recv[s, 0] = gram_send[s]
        send_parts(lambda i: gram_send.at[s], lambda i: gram_recv.at[s, i], 7 + s, 1)

    def finish_gram(s):
        wait_on(gram_recv.at[s, rest], part_rsem.at[7 + s])
        return jnp.sum(gram_recv[s], axis=0)

    def sym(g):
        return 0.5 * (g + g.T)

    loads = jnp.concatenate([bload_ref[:, k, :] for k in range(ncase)], axis=1)
    lifted = apply_tables(inv_tab, loads)
    inv_keep[...] = lifted
    condensed = -apply_tables(coup_tab, lifted)
    start_far(0, slot_pick, tall(condensed[pd:]), 1)
    own = jnp.concatenate([pload_ref[:, k, :] for k in range(ncase)], axis=0)
    own = own + pick(tall(condensed[:pd]), near_out)
    wait_on(ask_recv.at[rest], part_rsem.at[6])
    port_lane = lax.broadcasted_iota(jnp.int32, (slots, nport), 1).astype(F32)
    asked_pick = jnp.where(ask_recv[...].reshape(slots, nport) == port_lane, 1.0, 0.0).astype(BF16)
    base = own + finish_far(0, asked_pick)
    publish(0, base)

    def spread_start(e, field):
        start_far(e, asked_pick, field, -1)
        return pick(field, near_in)

    def spread_finish(e, near):
        far = finish_far(e, slot_pick)
        return jnp.concatenate([wide(near, pd), wide(far, pd)], axis=0)

    def operate_start(e, near):
        y = apply_tables(schur_tab, spread_finish(e, near)) * stiff
        start_far(e + 1, slot_pick, tall(y[pd:]), 1)
        return pick(tall(y[:pd]), near_out)

    near = spread_start(1, base)
    own = operate_start(1, near)
    first = own + finish_far(2, asked_pick)
    publish(1, first)
    near = spread_start(3, first)
    collect(0)
    own = operate_start(3, near)
    collect(1)
    pair = rows_all[0:2 * allcase, :]
    start_gram(0, exact(pair, pair, NT))
    second = own + finish_far(4, asked_pick)
    publish(2, second)

    n = allcase
    grams = finish_gram(0)
    g00 = sym(grams[0:n, 0:n])
    g01 = sym(grams[0:n, n:2 * n])
    g11 = sym(grams[n:2 * n, n:2 * n])
    step1 = gauss_solve(g01, g00)
    cross = exact(g01, step1)
    g1 = sym(g00 - cross - cross.T + exact(step1, exact(g11, step1), TN))
    turn = gauss_solve(g00, g1)
    eye = jnp.where(
        lax.broadcasted_iota(jnp.int32, (n, n), 0) == lax.broadcasted_iota(jnp.int32, (n, n), 1),
        1.0,
        0.0,
    )
    lead = turn + eye
    mixed = exact(lead, exact(g11, step1), TN)
    known = exact(lead, exact(g01, lead), TN) - mixed - mixed.T

    collect(2)
    start_gram(1, exact(rows_all[n:2 * n, :], rows_all[2 * n:3 * n, :], NT))
    g12 = sym(finish_gram(1)[0:n, 0:n])
    curve = sym(known + exact(step1, exact(g12, step1), TN))
    step2 = gauss_solve(curve, g1)
    alpha = step1 + exact(lead, step2)
    beta = exact(step1, step2)
    at = alpha.T[0:ncase]
    bt = beta.T[0:ncase]
    zero = jnp.zeros_like(at)
    coefs = jnp.concatenate(
        [
            jnp.concatenate([at, -bt, zero], axis=1),
            jnp.concatenate([zero, -at, bt], axis=1),
        ],
        axis=0,
    )
    ctop, clow = split(coefs)
    both = jnp.concatenate([ctop, clow], axis=0)
    vtop, vlow = split(rows_all[...])
    part_a = mm(both, vtop)
    mixed_rows = part_a[0:2 * ncase] + part_a[2 * ncase:] + mm(ctop, vlow)
    for d in range(pd):
        cols = slice(d * nport, (d + 1) * nport)
        sol_ref[d] = mixed_rows[0:ncase, cols]
        res_ref[d] = nat[0, d] + mixed_rows[ncase:, cols]

    answer = jnp.concatenate([sol_ref[:, k, :] for k in range(ncase)], axis=0)
    near = spread_start(5, answer)
    scaled = inv_keep[...] / stiff
    back = scaled - apply_tables(red_tab, spread_finish(5, near))
    for k in range(ncase):
        bub_ref[:, k, :] = back[:, k * ncomp:(k + 1) * ncomp]

    wait_on(ask_send.at[rest], part_ssem.at[6])
    for e in range(6):
        wait_on(far_send.at[e, rest], part_ssem.at[e])
    for s in range(2):
        wait_on(gram_recv.at[s, rest], part_ssem.at[7 + s])
    for f in range(3):
        wait_on(gath.at[f, pl.ds(1, nq - 1)], case_ssem.at[f])


def local(
    comp_type,
    stiffness,
    near_port,
    far_owner,
    far_port,
    bubble_load,
    port_load,
    bubble_inverse,
    coupling,
    port_block,
):
    npy = lax.axis_size("py")
    parts = lax.axis_size("px") * npy
    nq = lax.axis_size("case")
    ncomp = comp_type.shape[0]
    modes, ncase, _ = bubble_load.shape
    pd, _, nport = port_load.shape
    cap = 3 * ncomp // (2 * parts)
    depth = -(-cap // 8) * 8
    allcase = nq * ncase
    idx = jnp.stack([comp_type, near_port, far_owner[:, 0], far_port])
    vmem = pl.BlockSpec(memory_space=pltpu.VMEM)

    def body(*refs):
        kernel((parts, npy, nq, depth), *refs)

    return pl.pallas_call(
        body,
        out_shape=(
            jax.ShapeDtypeStruct(port_load.shape, F32),
            jax.ShapeDtypeStruct(port_load.shape, F32),
            jax.ShapeDtypeStruct(bubble_load.shape, F32),
        ),
        in_specs=[vmem] * 7,
        out_specs=(vmem, vmem, vmem),
        scratch_shapes=[
            pltpu.VMEM((parts, depth, nport), F32),
            pltpu.VMEM((parts, depth, nport), F32),
            pltpu.VMEM((6, parts, depth, ncase * pd), F32),
            pltpu.VMEM((6, parts, depth, ncase * pd), F32),
            pltpu.VMEM((3, pd, ncase, nport), F32),
            pltpu.VMEM((3, nq, pd, ncase, nport), F32),
            pltpu.VMEM((3 * allcase, pd * nport), F32),
            pltpu.VMEM((2, 2 * allcase, 128), F32),
            pltpu.VMEM((2, parts, 2 * allcase, 128), F32),
            pltpu.VMEM((modes, ncase * ncomp), F32),
            pltpu.SemaphoreType.DMA((9,)),
            pltpu.SemaphoreType.DMA((9,)),
            pltpu.SemaphoreType.DMA((3,)),
            pltpu.SemaphoreType.DMA((3,)),
        ],
        compiler_params=pltpu.CompilerParams(
            collective_id=0, has_side_effects=True, vmem_limit_bytes=60 * 1024 * 1024
        ),
        name="condensed_solve",
    )(
        idx,
        stiffness.reshape(1, ncomp),
        bubble_load,
        port_load,
        bubble_inverse,
        coupling,
        port_block,
    )


def solution(mesh):
    placed = (
        P(("px", "py")),
        P(("px", "py")),
        P(("px", "py")),
        P(("px", "py"), None),
        P(("px", "py")),
        P(None, "case", ("px", "py")),
        P(None, "case", ("px", "py")),
        P(),
        P(),
        P(),
    )
    return jax.shard_map(
        local,
        mesh=mesh,
        in_specs=placed,
        out_specs=(
            P(None, "case", ("px", "py")),
            P(None, "case", ("px", "py")),
            P(None, "case", ("px", "py")),
        ),
        check_vma=False,
    )
```

```python
import jax
import jax.numpy as jnp
from jax import lax
from jax.experimental import pallas as pl
from jax.experimental.pallas import tpu as pltpu
from jax.sharding import PartitionSpec as P

HIGH = lax.Precision.HIGHEST
F32 = jnp.float32
BF16 = jnp.bfloat16
MESH = pl.DeviceIdType.MESH
NT = (((1,), (1,)), ((), ()))
TN = (((0,), (0,)), ((), ()))


def split(x):
    top = x.astype(BF16)
    return top, (x - top.astype(F32)).astype(BF16)


def mm(a, b):
    return jnp.dot(a, b, preferred_element_type=F32)


def exact(a, b, dims=(((1,), (0,)), ((), ()))):
    return lax.dot_general(a, b, dims, precision=HIGH, preferred_element_type=F32)


def gauss_solve(matrix, target):
    n = matrix.shape[0]
    aug = jnp.concatenate([matrix, target], axis=1)
    rows = lax.broadcasted_iota(jnp.int32, aug.shape, 0)
    for j in range(n):
        row = aug[j:j + 1, :]
        row = row / row[:, j:j + 1]
        aug = jnp.where(rows == j, row, aug - aug[:, j:j + 1] * row)
    return aug[:, n:]


def kernel(
    sizes,
    idx_ref,
    stiff_ref,
    bload_ref,
    pload_ref,
    binv_ref,
    coup_ref,
    pblock_ref,
    sol_ref,
    res_ref,
    bub_ref,
    ask_send,
    ask_recv,
    far_send,
    far_recv,
    nat,
    gath,
    rows_all,
    pair_send,
    pair_recv,
    last_send,
    last_recv,
    inv_keep,
    nat_far,
    part_ssem,
    part_rsem,
    case_ssem,
    case_rsem,
):
    gram_refs = ((pair_send, pair_recv), (last_send, last_recv))
    parts, npy, nq, depth = sizes
    kinds = binv_ref.shape[0]
    modes, ncase, ncomp = bload_ref.shape
    pd = pload_ref.shape[0]
    nport = pload_ref.shape[2]
    slots = parts * depth
    allcase = nq * ncase
    my_x, my_y, my_c = lax.axis_index("px"), lax.axis_index("py"), lax.axis_index("case")
    me = my_x * npy + my_y

    def part_id(step):
        other = lax.rem(me + step + parts, parts)
        return (other // npy, lax.rem(other, npy), my_c)

    def case_id(step):
        return (my_x, my_y, lax.rem(my_c + step, nq))

    barrier = pltpu.get_barrier_semaphore()

    def greet_part(i, _):
        pl.semaphore_signal(barrier, inc=1, device_id=part_id(i), device_id_type=MESH)
        return 0

    lax.fori_loop(1, parts, greet_part, 0)
    for i in range(1, nq):
        pl.semaphore_signal(barrier, inc=1, device_id=case_id(i), device_id_type=MESH)

    kind_row = idx_ref[0:1, :]
    near_row = idx_ref[1:2, :]
    owner_row = idx_ref[2:3, :]
    far_row = idx_ref[3:4, :]

    def as_column(row):
        return jnp.broadcast_to(row.astype(F32), (ncomp, ncomp)).T

    sub = lax.broadcasted_iota(jnp.int32, (ncomp, ncomp), 0)
    lane = lax.broadcasted_iota(jnp.int32, (ncomp, ncomp), 1)
    same = (as_column(owner_row) == owner_row.astype(F32)) & (sub < lane)
    rank = jnp.sum(jnp.where(same, 1.0, 0.0), axis=0, keepdims=True).astype(jnp.int32)
    slot_row = lax.rem(owner_row - me + parts, parts) * depth + rank
    slot_sub = lax.broadcasted_iota(jnp.int32, (slots, ncomp), 0)
    slot_f = jnp.where(slot_sub == slot_row, 1.0, 0.0)
    slot_pick = slot_f.astype(BF16)
    wanted = jnp.sum(slot_f * (far_row + 1).astype(F32), axis=1, keepdims=True) - 1.0
    wanted = jnp.broadcast_to(wanted, (slots, nport)).reshape(parts, depth, nport)
    ask_send[...] = wanted
    ask_recv[0] = wanted[0]
    near_in = jnp.where(sub == near_row, 1.0, 0.0).astype(BF16)
    near_out = jnp.where(lane.astype(F32) == as_column(near_row), 1.0, 0.0).astype(BF16)

    pl.semaphore_wait(barrier, parts - 1 + nq - 1)

    def send_parts(src, dst, e, sign):
        def body(i, _):
            pltpu.make_async_remote_copy(
                src_ref=src(i),
                dst_ref=dst(i),
                send_sem=part_ssem.at[e],
                recv_sem=part_rsem.at[e],
                device_id=part_id(i if sign > 0 else -i),
                device_id_type=MESH,
            ).start()
            return 0

        if parts <= 8:
            for i in range(1, parts):
                body(i, 0)
        else:
            lax.fori_loop(1, parts, body, 0)

    def wait_on(ref, sem):
        pltpu.make_async_copy(ref, ref, sem).wait()

    rest = pl.ds(1, parts - 1)
    send_parts(lambda i: ask_send.at[i], lambda i: ask_recv.at[i], 6, 1)

    red_t = [exact(binv_ref[t], coup_ref[t], TN) for t in range(kinds)]
    schur = [pblock_ref[t] - exact(red_t[t], coup_ref[t], TN) for t in range(kinds)]
    inv_tab = split(jnp.concatenate([binv_ref[t] for t in range(kinds)], axis=1))
    coup_tab = split(jnp.concatenate([coup_ref[t].T for t in range(kinds)], axis=1))
    schur_tab = split(jnp.concatenate(schur, axis=1))
    red_tab = split(jnp.concatenate(red_t, axis=1))

    def tile_cases(row):
        return jnp.concatenate([row] * ncase, axis=1)

    stiff = tile_cases(stiff_ref[...])
    kind_all = tile_cases(kind_row)
    masks = [jnp.where(kind_all == t, 1.0, 0.0).astype(BF16) for t in range(kinds)]

    def apply_tables(tab, x):
        top, low = split(x)
        xt = jnp.concatenate([top * m for m in masks], axis=0)
        xl = jnp.concatenate([low * m for m in masks], axis=0)
        return mm(tab[0], xt) + mm(tab[0], xl) + mm(tab[1], xt)

    def wide(field, rows):
        return jnp.concatenate(
            [field[k * rows:(k + 1) * rows] for k in range(ncase)], axis=1
        )

    def tall(x):
        return jnp.concatenate(
            [x[:, k * ncomp:(k + 1) * ncomp] for k in range(ncase)], axis=0
        )

    def pick(x, onehot):
        top, low = split(x)
        return mm(jnp.concatenate([top, low], axis=1), jnp.concatenate([onehot, onehot], axis=0))

    def start_far(e, onehot, x, sign):
        top, low = split(x)
        out = lax.dot_general(
            jnp.concatenate([onehot, onehot], axis=1),
            jnp.concatenate([top, low], axis=1),
            NT,
            preferred_element_type=F32,
        ).reshape(parts, depth, x.shape[0])
        far_send[e] = out
        far_recv[e, 0] = out[0]
        send_parts(lambda i: far_send.at[e, i], lambda i: far_recv.at[e, i], e, sign)

    def finish_far(e, onehot):
        wait_on(far_recv.at[e, rest], part_rsem.at[e])
        got = far_recv[e].reshape(slots, ncase * pd).T
        top, low = split(got)
        return mm(top, onehot) + mm(low, onehot)

    def publish(f, field):
        for k in range(ncase):
            nat[f, :, k, :] = field[k * pd:(k + 1) * pd]
        for i in range(1, nq):
            pltpu.make_async_remote_copy(
                src_ref=nat.at[f],
                dst_ref=gath.at[f, i],
                send_sem=case_ssem.at[f],
                recv_sem=case_rsem.at[f],
                device_id=case_id(i),
                device_id_type=MESH,
            ).start()

    def collect(f):
        wait_on(gath.at[f, pl.ds(1, nq - 1)], case_rsem.at[f])

        def body(d, _):
            cols = pl.ds(pl.multiple_of(d * nport, nport), nport)
            rows_all[pl.ds(f * allcase, ncase), cols] = nat[f, d]
            for q in range(1, nq):
                rows_all[pl.ds(f * allcase + q * ncase, ncase), cols] = gath[f, q, d]
            return 0

        lax.fori_loop(0, pd, body, 0)

    def start_gram(s, value):
        sent, got = gram_refs[s]
        folded = jnp.concatenate(
            [value[8 * r:8 * r + 8] for r in range(value.shape[0] // 8)], axis=1
        )
        sent[...] = folded
        got[0] = folded
        send_parts(lambda i: sent, lambda i: got.at[i], 7 + s, 1)

    def finish_gram(s):
        got = gram_refs[s][1]
        wait_on(got.at[rest], part_rsem.at[7 + s])
        total = jnp.sum(got[...], axis=0)
        return jnp.concatenate(
            [total[:, allcase * r:allcase * (r + 1)] for r in range(total.shape[1] // allcase)],
            axis=0,
        )

    def sym(g):
        return 0.5 * (g + g.T)

    loads = jnp.concatenate([bload_ref[:, k, :] for k in range(ncase)], axis=1)
    lifted = apply_tables(inv_tab, loads)
    inv_keep[...] = lifted
    condensed = -apply_tables(coup_tab, lifted)
    start_far(0, slot_pick, tall(condensed[pd:]), 1)
    own = jnp.concatenate([pload_ref[:, k, :] for k in range(ncase)], axis=0)
    own = own + pick(tall(condensed[:pd]), near_out)
    wait_on(ask_recv.at[rest], part_rsem.at[6])
    port_lane = lax.broadcasted_iota(jnp.int32, (slots, nport), 1).astype(F32)
    asked_pick = jnp.where(ask_recv[...].reshape(slots, nport) == port_lane, 1.0, 0.0).astype(BF16)
    base = own + finish_far(0, asked_pick)
    publish(0, base)

    def spread_start(e, field):
        start_far(e, asked_pick, field, -1)
        return pick(field, near_in)

    def spread_finish(e, near):
        far = finish_far(e, slot_pick)
        publish(3 + e // 2, far)
        return jnp.concatenate([wide(near, pd), wide(far, pd)], axis=0)

    def operate_start(e, near):
        y = apply_tables(schur_tab, spread_finish(e, near)) * stiff
        start_far(e + 1, slot_pick, tall(y[pd:]), 1)
        return pick(tall(y[:pd]), near_out)

    near = spread_start(1, base)
    own = operate_start(1, near)
    first = own + finish_far(2, asked_pick)
    publish(1, first)
    near = spread_start(3, first)
    collect(0)
    own = operate_start(3, near)
    collect(1)
    pair = rows_all[0:2 * allcase, :]
    square = exact(pair, pair, NT)
    start_gram(0, jnp.concatenate([square[0:allcase, 0:allcase], square[0:allcase, allcase:], square[allcase:, allcase:]], axis=0))
    second = own + finish_far(4, asked_pick)
    publish(2, second)

    n = allcase
    grams = finish_gram(0)
    g00 = sym(grams[0:n])
    g01 = sym(grams[n:2 * n])
    g11 = sym(grams[2 * n:3 * n])
    step1 = gauss_solve(g01, g00)
    cross = exact(g01, step1)
    g1 = sym(g00 - cross - cross.T + exact(step1, exact(g11, step1), TN))
    turn = gauss_solve(g00, g1)
    eye = jnp.where(
        lax.broadcasted_iota(jnp.int32, (n, n), 0) == lax.broadcasted_iota(jnp.int32, (n, n), 1),
        1.0,
        0.0,
    )
    lead = turn + eye
    mixed = exact(lead, exact(g11, step1), TN)
    known = exact(lead, exact(g01, lead), TN) - mixed - mixed.T

    collect(2)
    start_gram(1, exact(rows_all[n:2 * n, :], rows_all[2 * n:3 * n, :], NT))
    g12 = sym(finish_gram(1))
    curve = sym(known + exact(step1, exact(g12, step1), TN))
    step2 = gauss_solve(curve, g1)
    alpha = step1 + exact(lead, step2)
    beta = exact(step1, step2)
    at = alpha.T[0:ncase]
    bt = beta.T[0:ncase]
    zero = jnp.zeros_like(at)
    coefs = jnp.concatenate(
        [
            jnp.concatenate([at, -bt, zero], axis=1),
            jnp.concatenate([zero, -at, bt], axis=1),
        ],
        axis=0,
    )
    ctop, clow = split(coefs)
    both = jnp.concatenate([ctop, clow], axis=0)
    vtop, vlow = split(rows_all[0:3 * allcase, :])
    part_a = mm(both, vtop)
    mixed_rows = part_a[0:2 * ncase] + part_a[2 * ncase:] + mm(ctop, vlow)
    for d in range(pd):
        cols = slice(d * nport, (d + 1) * nport)
        sol_ref[d] = mixed_rows[0:ncase, cols]
        res_ref[d] = nat[0, d] + mixed_rows[ncase:, cols]

    answer = jnp.concatenate([sol_ref[:, k, :] for k in range(ncase)], axis=0)
    collect(3)
    collect(4)
    ftop, flow = split(rows_all[3 * allcase:, :])
    lead_a = jnp.concatenate([ctop[0:ncase, 0:2 * n], clow[0:ncase, 0:2 * n]], axis=0)
    part_f = mm(lead_a, ftop)
    far_rows = part_f[0:ncase] + part_f[ncase:] + mm(ctop[0:ncase, 0:2 * n], flow)
    for d in range(pd):
        nat_far[d] = far_rows[:, d * nport:(d + 1) * nport]
    near = wide(pick(answer, near_in), pd)
    ends = jnp.concatenate(
        [near, jnp.concatenate([nat_far[:, k, :] for k in range(ncase)], axis=1)], axis=0
    )
    scaled = inv_keep[...] / stiff
    back = scaled - apply_tables(red_tab, ends)
    for k in range(ncase):
        bub_ref[:, k, :] = back[:, k * ncomp:(k + 1) * ncomp]

    wait_on(ask_send.at[rest], part_ssem.at[6])
    for e in range(5):
        wait_on(far_send.at[e, rest], part_ssem.at[e])
    for s in range(2):
        wait_on(gram_refs[s][1].at[rest], part_ssem.at[7 + s])
    for f in range(5):
        wait_on(gath.at[f, pl.ds(1, nq - 1)], case_ssem.at[f])


def local(
    comp_type,
    stiffness,
    near_port,
    far_owner,
    far_port,
    bubble_load,
    port_load,
    bubble_inverse,
    coupling,
    port_block,
):
    npy = lax.axis_size("py")
    parts = lax.axis_size("px") * npy
    nq = lax.axis_size("case")
    ncomp = comp_type.shape[0]
    modes, ncase, _ = bubble_load.shape
    pd, _, nport = port_load.shape
    cap = 3 * ncomp // (2 * parts)
    depth = -(-cap // 8) * 8
    allcase = nq * ncase
    idx = jnp.stack([comp_type, near_port, far_owner[:, 0], far_port])
    vmem = pl.BlockSpec(memory_space=pltpu.VMEM)

    def body(*refs):
        kernel((parts, npy, nq, depth), *refs)

    return pl.pallas_call(
        body,
        out_shape=(
            jax.ShapeDtypeStruct(port_load.shape, F32),
            jax.ShapeDtypeStruct(port_load.shape, F32),
            jax.ShapeDtypeStruct(bubble_load.shape, F32),
        ),
        in_specs=[vmem] * 7,
        out_specs=(vmem, vmem, vmem),
        scratch_shapes=[
            pltpu.VMEM((parts, depth, nport), F32),
            pltpu.VMEM((parts, depth, nport), F32),
            pltpu.VMEM((5, parts, depth, ncase * pd), F32),
            pltpu.VMEM((5, parts, depth, ncase * pd), F32),
            pltpu.VMEM((5, pd, ncase, nport), F32),
            pltpu.VMEM((5, nq, pd, ncase, nport), F32),
            pltpu.VMEM((5 * allcase, pd * nport), F32),
            pltpu.VMEM((8, 3 * allcase * allcase // 8), F32),
            pltpu.VMEM((parts, 8, 3 * allcase * allcase // 8), F32),
            pltpu.VMEM((8, allcase * allcase // 8), F32),
            pltpu.VMEM((parts, 8, allcase * allcase // 8), F32),
            pltpu.VMEM((modes, ncase * ncomp), F32),
            pltpu.VMEM((pd, ncase, nport), F32),
            pltpu.SemaphoreType.DMA((9,)),
            pltpu.SemaphoreType.DMA((9,)),
            pltpu.SemaphoreType.DMA((5,)),
            pltpu.SemaphoreType.DMA((5,)),
        ],
        compiler_params=pltpu.CompilerParams(
            collective_id=0, has_side_effects=True, vmem_limit_bytes=60 * 1024 * 1024
        ),
        name="condensed_solve",
    )(
        idx,
        stiffness.reshape(1, ncomp),
        bubble_load,
        port_load,
        bubble_inverse,
        jnp.swapaxes(coupling, 1, 2),
        port_block,
    )


def solution(mesh):
    placed = (
        P(("px", "py")),
        P(("px", "py")),
        P(("px", "py")),
        P(("px", "py"), None),
        P(("px", "py")),
        P(None, "case", ("px", "py")),
        P(None, "case", ("px", "py")),
        P(),
        P(),
        P(),
    )
    return jax.shard_map(
        local,
        mesh=mesh,
        in_specs=placed,
        out_specs=(
            P(None, "case", ("px", "py")),
            P(None, "case", ("px", "py")),
            P(None, "case", ("px", "py")),
        ),
        check_vma=False,
    )
```

```python
import jax
import jax.numpy as jnp
from jax import lax
from jax.experimental import pallas as pl
from jax.experimental.pallas import tpu as pltpu
from jax.sharding import PartitionSpec as P

HIGH = lax.Precision.HIGHEST
F32 = jnp.float32
BF16 = jnp.bfloat16
MESH = pl.DeviceIdType.MESH
NT = (((1,), (1,)), ((), ()))
TN = (((0,), (0,)), ((), ()))


def split(x):
    top = x.astype(BF16)
    return top, (x - top.astype(F32)).astype(BF16)


def mm(a, b):
    return jnp.dot(a, b, preferred_element_type=F32)


def exact(a, b, dims=(((1,), (0,)), ((), ()))):
    return lax.dot_general(a, b, dims, precision=HIGH, preferred_element_type=F32)


def gauss_solve(matrix, target):
    n = matrix.shape[0]
    aug = jnp.concatenate([matrix, target], axis=1)
    rows = lax.broadcasted_iota(jnp.int32, aug.shape, 0)
    for j in range(n):
        row = aug[j:j + 1, :]
        row = row / row[:, j:j + 1]
        aug = jnp.where(rows == j, row, aug - aug[:, j:j + 1] * row)
    return aug[:, n:]


def kernel(
    sizes,
    idx_ref,
    stiff_ref,
    bload_ref,
    pload_ref,
    binv_ref,
    coup_ref,
    pblock_ref,
    sol_ref,
    res_ref,
    bub_ref,
    ask_send,
    ask_recv,
    far_send,
    far_recv,
    nat,
    gath,
    rows_all,
    pair_send,
    pair_recv,
    last_send,
    last_recv,
    inv_keep,
    nat_far,
    part_ssem,
    part_rsem,
    case_ssem,
    case_rsem,
):
    gram_refs = ((pair_send, pair_recv), (last_send, last_recv))
    parts, npy, nq, depth, width, chunks = sizes
    kinds = binv_ref.shape[0]
    modes, ncase, ncomp = bload_ref.shape
    pd = pload_ref.shape[0]
    nport = pload_ref.shape[2]
    slots = parts * depth
    allcase = nq * ncase
    my_x, my_y, my_c = lax.axis_index("px"), lax.axis_index("py"), lax.axis_index("case")
    me = my_x * npy + my_y

    def part_id(step):
        other = lax.rem(me + step + parts, parts)
        return (other // npy, lax.rem(other, npy), my_c)

    def case_id(step):
        if nq == 4:
            other = my_c + (step % 2) * (1 - 2 * lax.rem(my_c, 2))
            other = other + (step // 2) * (2 - 4 * (my_c // 2))
        else:
            other = lax.rem(my_c + step, nq)
        return (my_x, my_y, other)

    direct = (1, 2) if nq == 4 else tuple(range(1, nq))

    barrier = pltpu.get_barrier_semaphore()

    def greet_part(i, _):
        pl.semaphore_signal(barrier, inc=1, device_id=part_id(i), device_id_type=MESH)
        return 0

    lax.fori_loop(1, parts, greet_part, 0)
    for i in range(1, nq):
        pl.semaphore_signal(barrier, inc=1, device_id=case_id(i), device_id_type=MESH)

    kind_row = idx_ref[0:1, :]
    near_row = idx_ref[1:2, :]
    owner_row = idx_ref[2:3, :]
    far_row = idx_ref[3:4, :]

    def as_column(row):
        return jnp.broadcast_to(row.astype(F32), (ncomp, ncomp)).T

    sub = lax.broadcasted_iota(jnp.int32, (ncomp, ncomp), 0)
    lane = lax.broadcasted_iota(jnp.int32, (ncomp, ncomp), 1)
    same = (as_column(owner_row) == owner_row.astype(F32)) & (sub < lane)
    rank = jnp.sum(jnp.where(same, 1.0, 0.0), axis=0, keepdims=True).astype(jnp.int32)
    slot_row = lax.rem(owner_row - me + parts, parts) * depth + rank
    slot_sub = lax.broadcasted_iota(jnp.int32, (slots, ncomp), 0)
    slot_f = jnp.where(slot_sub == slot_row, 1.0, 0.0)
    slot_pick = slot_f.astype(BF16)
    wanted = jnp.sum(slot_f * (far_row + 1).astype(F32), axis=1, keepdims=True) - 1.0
    wanted = jnp.broadcast_to(wanted, (slots, nport)).reshape(parts, depth, nport)
    ask_send[...] = wanted
    ask_recv[0] = wanted[0]
    near_in = jnp.where(sub == near_row, 1.0, 0.0).astype(BF16)
    near_out = jnp.where(lane.astype(F32) == as_column(near_row), 1.0, 0.0).astype(BF16)

    pl.semaphore_wait(barrier, parts - 1 + nq - 1)

    def send_parts(src, dst, e, sign):
        def body(i, _):
            pltpu.make_async_remote_copy(
                src_ref=src(i),
                dst_ref=dst(i),
                send_sem=part_ssem.at[e],
                recv_sem=part_rsem.at[e],
                device_id=part_id(i if sign > 0 else -i),
                device_id_type=MESH,
            ).start()
            return 0

        if parts <= 8:
            for i in range(1, parts):
                body(i, 0)
        else:
            lax.fori_loop(1, parts, body, 0)

    def wait_on(ref, sem):
        pltpu.make_async_copy(ref, ref, sem).wait()

    rest = pl.ds(1, parts - 1)
    send_parts(lambda i: ask_send.at[i], lambda i: ask_recv.at[i], 0, 1)

    red_t = [exact(binv_ref[t], coup_ref[t], TN) for t in range(kinds)]
    schur = [pblock_ref[t] - exact(red_t[t], coup_ref[t], TN) for t in range(kinds)]
    inv_tab = split(jnp.concatenate([binv_ref[t] for t in range(kinds)], axis=1))
    coup_tab = split(jnp.concatenate([coup_ref[t].T for t in range(kinds)], axis=1))
    schur_tab = split(jnp.concatenate(schur, axis=1))
    red_tab = split(jnp.concatenate(red_t, axis=1))

    def tile_cases(row):
        return jnp.concatenate([row] * ncase, axis=1)

    stiff = tile_cases(stiff_ref[...])
    kind_all = tile_cases(kind_row)
    masks = [jnp.where(kind_all == t, 1.0, 0.0).astype(BF16) for t in range(kinds)]

    def apply_tables(tab, x):
        top, low = split(x)
        lanes = x.shape[1]
        xt = jnp.concatenate([top * m[:, :lanes] for m in masks], axis=0)
        xl = jnp.concatenate([low * m[:, :lanes] for m in masks], axis=0)
        return mm(tab[0], xt) + mm(tab[0], xl) + mm(tab[1], xt)

    def wide(field, rows):
        return jnp.concatenate(
            [field[k * rows:(k + 1) * rows] for k in range(field.shape[0] // rows)], axis=1
        )

    def tall(x):
        return jnp.concatenate(
            [x[:, k * ncomp:(k + 1) * ncomp] for k in range(x.shape[1] // ncomp)], axis=0
        )

    def pick(x, onehot):
        top, low = split(x)
        return mm(jnp.concatenate([top, low], axis=1), jnp.concatenate([onehot, onehot], axis=0))

    def start_far(e, j, onehot, x, sign):
        top, low = split(x)
        out = lax.dot_general(
            jnp.concatenate([onehot, onehot], axis=1),
            jnp.concatenate([top, low], axis=1),
            NT,
            preferred_element_type=F32,
        ).reshape(parts, depth, width)
        far_send[e, j] = out
        far_recv[e, j, 0] = out[0]
        send_parts(
            lambda i: far_send.at[e, j, i], lambda i: far_recv.at[e, j, i], 3 + e * chunks + j, sign
        )

    def finish_far(e, j, onehot):
        wait_on(far_recv.at[e, j, rest], part_rsem.at[3 + e * chunks + j])
        got = far_recv[e, j].reshape(slots, width).T
        top, low = split(got)
        return mm(top, onehot) + mm(low, onehot)

    def send_case(f, src, block, step):
        pltpu.make_async_remote_copy(
            src_ref=src,
            dst_ref=gath.at[f, block],
            send_sem=case_ssem.at[f, block],
            recv_sem=case_rsem.at[f, block],
            device_id=case_id(step),
            device_id_type=MESH,
        ).start()

    def publish(f, field):
        for k in range(ncase):
            nat[f, :, k, :] = field[k * pd:(k + 1) * pd]
        for i in reversed(direct):
            send_case(f, nat.at[f], i, i)

    def forward(f):
        if nq == 4:
            wait_on(gath.at[f, 2], case_rsem.at[f, 2])
            send_case(f, gath.at[f, 2], 3, 1)

    def collect(f):
        for i in range(1, nq):
            if nq != 4 or i != 2:
                wait_on(gath.at[f, i], case_rsem.at[f, i])

        def body(d, _):
            cols = pl.ds(pl.multiple_of(d * nport, nport), nport)
            rows_all[pl.ds(f * allcase, ncase), cols] = nat[f, d]
            for q in range(1, nq):
                rows_all[pl.ds(f * allcase + q * ncase, ncase), cols] = gath[f, q, d]
            return 0

        lax.fori_loop(0, pd, body, 0, unroll=4)

    def start_gram(s, value):
        sent, got = gram_refs[s]
        folded = jnp.concatenate(
            [value[8 * r:8 * r + 8] for r in range(value.shape[0] // 8)], axis=1
        )
        sent[...] = folded
        got[0] = folded
        send_parts(lambda i: sent, lambda i: got.at[i], 1 + s, 1)

    def finish_gram(s):
        got = gram_refs[s][1]
        wait_on(got.at[rest], part_rsem.at[1 + s])
        total = jnp.sum(got[...], axis=0)
        return jnp.concatenate(
            [total[:, allcase * r:allcase * (r + 1)] for r in range(total.shape[1] // allcase)],
            axis=0,
        )

    def sym(g):
        return 0.5 * (g + g.T)

    def part(x, j):
        return x[j * width:(j + 1) * width]

    loads = jnp.concatenate([bload_ref[:, k, :] for k in range(ncase)], axis=1)
    lifted = apply_tables(inv_tab, loads)
    inv_keep[...] = lifted
    condensed = -apply_tables(coup_tab, lifted)
    leaving = tall(condensed[pd:])
    for j in range(chunks):
        start_far(0, j, slot_pick, part(leaving, j), 1)
    own = jnp.concatenate([pload_ref[:, k, :] for k in range(ncase)], axis=0)
    own = own + pick(tall(condensed[:pd]), near_out)
    wait_on(ask_recv.at[rest], part_rsem.at[0])
    port_lane = lax.broadcasted_iota(jnp.int32, (slots, nport), 1).astype(F32)
    asked_pick = jnp.where(ask_recv[...].reshape(slots, nport) == port_lane, 1.0, 0.0).astype(BF16)

    def arrive(e, own, onward):
        pieces = []
        for j in range(chunks):
            piece = part(own, j) + finish_far(e, j, asked_pick)
            if onward:
                start_far(e + 1, j, asked_pick, piece, -1)
            pieces.append(piece)
        return jnp.concatenate(pieces, axis=0)

    def operate(e, near):
        cuts = [0, ((chunks - 1) * width) // pd, ncase] if chunks > 1 else [0, ncase]
        far, near_y, far_y, sent, have = None, None, None, 0, 0
        for a, b in zip(cuts[:-1], cuts[1:]):
            while have * width < b * pd:
                piece = finish_far(e, have, slot_pick)
                far = piece if far is None else jnp.concatenate([far, piece], axis=0)
                have += 1
            rows = slice(a * pd, b * pd)
            ends = jnp.concatenate([wide(near[rows], pd), wide(far[rows], pd)], axis=0)
            y = apply_tables(schur_tab, ends) * stiff[:, a * ncomp:b * ncomp]
            out = tall(y[pd:])
            far_y = out if far_y is None else jnp.concatenate([far_y, out], axis=0)
            out = tall(y[:pd])
            near_y = out if near_y is None else jnp.concatenate([near_y, out], axis=0)
            while (sent + 1) * width <= b * pd:
                start_far(e + 1, sent, slot_pick, part(far_y, sent), 1)
                sent += 1
        return far, pick(near_y, near_out)

    base = arrive(0, own, True)
    publish(0, base)
    far_base, own = operate(1, pick(base, near_in))
    publish(3, far_base)
    forward(0)
    first = arrive(2, own, True)
    publish(1, first)
    near = pick(first, near_in)
    forward(3)
    collect(0)
    far_first, own = operate(3, near)
    forward(1)
    publish(4, far_first)
    collect(1)
    pair = rows_all[0:2 * allcase, :]
    square = exact(pair, pair, NT)
    start_gram(0, jnp.concatenate([square[0:allcase, 0:allcase], square[0:allcase, allcase:], square[allcase:, allcase:]], axis=0))
    second = arrive(4, own, False)
    publish(2, second)
    forward(4)
    collect(3)

    n = allcase
    grams = finish_gram(0)
    g00 = sym(grams[0:n])
    g01 = sym(grams[n:2 * n])
    g11 = sym(grams[2 * n:3 * n])
    step1 = gauss_solve(g01, g00)
    forward(2)
    cross = exact(g01, step1)
    g1 = sym(g00 - cross - cross.T + exact(step1, exact(g11, step1), TN))
    turn = gauss_solve(g00, g1)
    eye = jnp.where(
        lax.broadcasted_iota(jnp.int32, (n, n), 0) == lax.broadcasted_iota(jnp.int32, (n, n), 1),
        1.0,
        0.0,
    )
    lead = turn + eye
    mixed = exact(lead, exact(g11, step1), TN)
    known = exact(lead, exact(g01, lead), TN) - mixed - mixed.T

    collect(4)
    collect(2)
    start_gram(1, exact(rows_all[n:2 * n, :], rows_all[2 * n:3 * n, :], NT))
    g12 = sym(finish_gram(1))
    curve = sym(known + exact(step1, exact(g12, step1), TN))
    step2 = gauss_solve(curve, g1)
    alpha = step1 + exact(lead, step2)
    beta = exact(step1, step2)
    at = alpha.T[0:ncase]
    bt = beta.T[0:ncase]
    zero = jnp.zeros_like(at)
    coefs = jnp.concatenate(
        [
            jnp.concatenate([at, -bt, zero], axis=1),
            jnp.concatenate([zero, -at, bt], axis=1),
        ],
        axis=0,
    )
    ctop, clow = split(coefs)
    both = jnp.concatenate([ctop, clow], axis=0)
    vtop, vlow = split(rows_all[0:3 * allcase, :])
    part_a = mm(both, vtop)
    mixed_rows = part_a[0:2 * ncase] + part_a[2 * ncase:] + mm(ctop, vlow)
    for d in range(pd):
        cols = slice(d * nport, (d + 1) * nport)
        sol_ref[d] = mixed_rows[0:ncase, cols]
        res_ref[d] = nat[0, d] + mixed_rows[ncase:, cols]

    answer = jnp.concatenate([sol_ref[:, k, :] for k in range(ncase)], axis=0)
    ftop, flow = split(rows_all[3 * allcase:, :])
    lead_a = jnp.concatenate([ctop[0:ncase, 0:2 * n], clow[0:ncase, 0:2 * n]], axis=0)
    part_f = mm(lead_a, ftop)
    far_rows = part_f[0:ncase] + part_f[ncase:] + mm(ctop[0:ncase, 0:2 * n], flow)
    for d in range(pd):
        nat_far[d] = far_rows[:, d * nport:(d + 1) * nport]
    near = wide(pick(answer, near_in), pd)
    ends = jnp.concatenate(
        [near, jnp.concatenate([nat_far[:, k, :] for k in range(ncase)], axis=1)], axis=0
    )
    scaled = inv_keep[...] / stiff
    back = scaled - apply_tables(red_tab, ends)
    for k in range(ncase):
        bub_ref[:, k, :] = back[:, k * ncomp:(k + 1) * ncomp]

    wait_on(ask_send.at[rest], part_ssem.at[0])
    for e in range(5):
        for j in range(chunks):
            wait_on(far_send.at[e, j, rest], part_ssem.at[3 + e * chunks + j])
    for s in range(2):
        wait_on(gram_refs[s][1].at[rest], part_ssem.at[1 + s])
    for f in range(5):
        for i in range(1, nq):
            wait_on(nat.at[f], case_ssem.at[f, i])


def local(
    comp_type,
    stiffness,
    near_port,
    far_owner,
    far_port,
    bubble_load,
    port_load,
    bubble_inverse,
    coupling,
    port_block,
):
    npy = lax.axis_size("py")
    parts = lax.axis_size("px") * npy
    nq = lax.axis_size("case")
    ncomp = comp_type.shape[0]
    modes, ncase, _ = bubble_load.shape
    pd, _, nport = port_load.shape
    cap = 3 * ncomp // (2 * parts)
    depth = -(-cap // 8) * 8
    allcase = nq * ncase
    width = 128 if (ncase * pd) % 128 == 0 else ncase * pd
    chunks = ncase * pd // width
    idx = jnp.stack([comp_type, near_port, far_owner[:, 0], far_port])
    vmem = pl.BlockSpec(memory_space=pltpu.VMEM)

    def body(*refs):
        kernel((parts, npy, nq, depth, width, chunks), *refs)

    return pl.pallas_call(
        body,
        out_shape=(
            jax.ShapeDtypeStruct(port_load.shape, F32),
            jax.ShapeDtypeStruct(port_load.shape, F32),
            jax.ShapeDtypeStruct(bubble_load.shape, F32),
        ),
        in_specs=[vmem] * 7,
        out_specs=(vmem, vmem, vmem),
        scratch_shapes=[
            pltpu.VMEM((parts, depth, nport), F32),
            pltpu.VMEM((parts, depth, nport), F32),
            pltpu.VMEM((5, chunks, parts, depth, width), F32),
            pltpu.VMEM((5, chunks, parts, depth, width), F32),
            pltpu.VMEM((5, pd, ncase, nport), F32),
            pltpu.VMEM((5, nq, pd, ncase, nport), F32),
            pltpu.VMEM((5 * allcase, pd * nport), F32),
            pltpu.VMEM((8, 3 * allcase * allcase // 8), F32),
            pltpu.VMEM((parts, 8, 3 * allcase * allcase // 8), F32),
            pltpu.VMEM((8, allcase * allcase // 8), F32),
            pltpu.VMEM((parts, 8, allcase * allcase // 8), F32),
            pltpu.VMEM((modes, ncase * ncomp), F32),
            pltpu.VMEM((pd, ncase, nport), F32),
            pltpu.SemaphoreType.DMA((3 + 5 * chunks,)),
            pltpu.SemaphoreType.DMA((3 + 5 * chunks,)),
            pltpu.SemaphoreType.DMA((5, nq)),
            pltpu.SemaphoreType.DMA((5, nq)),
        ],
        compiler_params=pltpu.CompilerParams(
            collective_id=0, has_side_effects=True, vmem_limit_bytes=60 * 1024 * 1024
        ),
        name="condensed_solve",
    )(
        idx,
        stiffness.reshape(1, ncomp),
        bubble_load,
        port_load,
        bubble_inverse,
        jnp.swapaxes(coupling, 1, 2),
        port_block,
    )


def solution(mesh):
    placed = (
        P(("px", "py")),
        P(("px", "py")),
        P(("px", "py")),
        P(("px", "py"), None),
        P(("px", "py")),
        P(None, "case", ("px", "py")),
        P(None, "case", ("px", "py")),
        P(),
        P(),
        P(),
    )
    return jax.shard_map(
        local,
        mesh=mesh,
        in_specs=placed,
        out_specs=(
            P(None, "case", ("px", "py")),
            P(None, "case", ("px", "py")),
            P(None, "case", ("px", "py")),
        ),
        check_vma=False,
    )
```

```python
import jax
import jax.numpy as jnp
from jax import lax
from jax.experimental import pallas as pl
from jax.experimental.pallas import tpu as pltpu
from jax.sharding import PartitionSpec as P

HIGH = lax.Precision.HIGHEST
F32 = jnp.float32
BF16 = jnp.bfloat16
MESH = pl.DeviceIdType.MESH
NT = (((1,), (1,)), ((), ()))
TN = (((0,), (0,)), ((), ()))


def split(x):
    top = x.astype(BF16)
    return top, (x - top.astype(F32)).astype(BF16)


def mm(a, b):
    return jnp.dot(a, b, preferred_element_type=F32)


def exact(a, b, dims=(((1,), (0,)), ((), ()))):
    return lax.dot_general(a, b, dims, precision=HIGH, preferred_element_type=F32)


def gauss_solve(matrix, target):
    n = matrix.shape[0]
    aug = jnp.concatenate([matrix, target], axis=1)
    rows = lax.broadcasted_iota(jnp.int32, aug.shape, 0)
    for j in range(n):
        row = aug[j:j + 1, :]
        row = row / row[:, j:j + 1]
        aug = jnp.where(rows == j, row, aug - aug[:, j:j + 1] * row)
    return aug[:, n:]


def kernel(
    sizes,
    idx_ref,
    stiff_ref,
    bload_ref,
    pload_ref,
    binv_ref,
    coup_ref,
    pblock_ref,
    sol_ref,
    res_ref,
    bub_ref,
    ask_send,
    ask_recv,
    far_send,
    far_recv,
    nat,
    gath,
    rows_all,
    pair_send,
    pair_recv,
    last_send,
    last_recv,
    inv_keep,
    nat_far,
    part_ssem,
    part_rsem,
    case_ssem,
    case_rsem,
):
    gram_refs = ((pair_send, pair_recv), (last_send, last_recv))
    parts, npy, nq, depth, width, chunks = sizes
    kinds = binv_ref.shape[0]
    modes, ncase, ncomp = bload_ref.shape
    pd = pload_ref.shape[0]
    nport = pload_ref.shape[2]
    slots = parts * depth
    allcase = nq * ncase
    my_x, my_y, my_c = lax.axis_index("px"), lax.axis_index("py"), lax.axis_index("case")
    me = my_x * npy + my_y

    def part_id(step):
        other = lax.rem(me + step + parts, parts)
        return (other // npy, lax.rem(other, npy), my_c)

    def case_id(step):
        if nq == 4:
            other = my_c + (step % 2) * (1 - 2 * lax.rem(my_c, 2))
            other = other + (step // 2) * (2 - 4 * (my_c // 2))
        else:
            other = lax.rem(my_c + step, nq)
        return (my_x, my_y, other)

    direct = (1, 2) if nq == 4 else tuple(range(1, nq))

    barrier = pltpu.get_barrier_semaphore()

    def greet_part(i, _):
        pl.semaphore_signal(barrier, inc=1, device_id=part_id(i), device_id_type=MESH)
        return 0

    lax.fori_loop(1, parts, greet_part, 0)
    for i in range(1, nq):
        pl.semaphore_signal(barrier, inc=1, device_id=case_id(i), device_id_type=MESH)

    kind_row = idx_ref[0:1, :]
    near_row = idx_ref[1:2, :]
    owner_row = idx_ref[2:3, :]
    far_row = idx_ref[3:4, :]

    def as_column(row):
        return jnp.broadcast_to(row.astype(F32), (ncomp, ncomp)).T

    sub = lax.broadcasted_iota(jnp.int32, (ncomp, ncomp), 0)
    lane = lax.broadcasted_iota(jnp.int32, (ncomp, ncomp), 1)
    same = (as_column(owner_row) == owner_row.astype(F32)) & (sub < lane)
    rank = jnp.sum(jnp.where(same, 1.0, 0.0), axis=0, keepdims=True).astype(jnp.int32)
    slot_row = lax.rem(owner_row - me + parts, parts) * depth + rank
    slot_sub = lax.broadcasted_iota(jnp.int32, (slots, ncomp), 0)
    slot_f = jnp.where(slot_sub == slot_row, 1.0, 0.0)
    slot_pick = slot_f.astype(BF16)
    wanted = jnp.sum(slot_f * (far_row + 1).astype(F32), axis=1, keepdims=True) - 1.0
    wanted = jnp.broadcast_to(wanted, (slots, nport)).reshape(parts, depth, nport)
    ask_send[...] = wanted
    ask_recv[0] = wanted[0]
    near_in = jnp.where(sub == near_row, 1.0, 0.0).astype(BF16)
    near_out = jnp.where(lane.astype(F32) == as_column(near_row), 1.0, 0.0).astype(BF16)

    pl.semaphore_wait(barrier, parts - 1 + nq - 1)

    def send_parts(src, dst, e, sign):
        def body(i, _):
            pltpu.make_async_remote_copy(
                src_ref=src(i),
                dst_ref=dst(i),
                send_sem=part_ssem.at[e],
                recv_sem=part_rsem.at[e],
                device_id=part_id(i if sign > 0 else -i),
                device_id_type=MESH,
            ).start()
            return 0

        if parts <= 8:
            for i in range(1, parts):
                body(i, 0)
        else:
            lax.fori_loop(1, parts, body, 0)

    def wait_on(ref, sem):
        pltpu.make_async_copy(ref, ref, sem).wait()

    rest = pl.ds(1, parts - 1)
    send_parts(lambda i: ask_send.at[i], lambda i: ask_recv.at[i], 0, 1)

    inv_tab = split(jnp.concatenate([binv_ref[t] for t in range(kinds)], axis=1))
    coup_tab = split(jnp.concatenate([coup_ref[t].T for t in range(kinds)], axis=1))

    def tile_cases(row):
        return jnp.concatenate([row] * ncase, axis=1)

    stiff = tile_cases(stiff_ref[...])
    kind_all = tile_cases(kind_row)
    masks = [jnp.where(kind_all == t, 1.0, 0.0).astype(BF16) for t in range(kinds)]

    def apply_tables(tab, x):
        top, low = split(x)
        lanes = x.shape[1]
        xt = jnp.concatenate([top * m[:, :lanes] for m in masks], axis=0)
        xl = jnp.concatenate([low * m[:, :lanes] for m in masks], axis=0)
        return mm(tab[0], xt) + mm(tab[0], xl) + mm(tab[1], xt)

    def wide(field, rows):
        return jnp.concatenate(
            [field[k * rows:(k + 1) * rows] for k in range(field.shape[0] // rows)], axis=1
        )

    def tall(x):
        return jnp.concatenate(
            [x[:, k * ncomp:(k + 1) * ncomp] for k in range(x.shape[1] // ncomp)], axis=0
        )

    def pick(x, onehot):
        top, low = split(x)
        return mm(jnp.concatenate([top, low], axis=1), jnp.concatenate([onehot, onehot], axis=0))

    def start_far(e, j, onehot, x, sign):
        top, low = split(x)
        out = lax.dot_general(
            jnp.concatenate([onehot, onehot], axis=1),
            jnp.concatenate([top, low], axis=1),
            NT,
            preferred_element_type=F32,
        ).reshape(parts, depth, width)
        far_send[e, j] = out
        far_recv[e, j, 0] = out[0]
        send_parts(
            lambda i: far_send.at[e, j, i], lambda i: far_recv.at[e, j, i], 3 + e * chunks + j, sign
        )

    def finish_far(e, j, onehot):
        wait_on(far_recv.at[e, j, rest], part_rsem.at[3 + e * chunks + j])
        got = far_recv[e, j].reshape(slots, width).T
        top, low = split(got)
        return mm(top, onehot) + mm(low, onehot)

    def send_case(f, src, block, step):
        pltpu.make_async_remote_copy(
            src_ref=src,
            dst_ref=gath.at[f, block],
            send_sem=case_ssem.at[f, block],
            recv_sem=case_rsem.at[f, block],
            device_id=case_id(step),
            device_id_type=MESH,
        ).start()

    def publish(f, field):
        for k in range(ncase):
            nat[f, :, k, :] = field[k * pd:(k + 1) * pd]
        for i in reversed(direct):
            send_case(f, nat.at[f], i, i)

    def forward(f):
        if nq == 4:
            wait_on(gath.at[f, 2], case_rsem.at[f, 2])
            send_case(f, gath.at[f, 2], 3, 1)

    def collect(f):
        for i in range(1, nq):
            if nq != 4 or i != 2:
                wait_on(gath.at[f, i], case_rsem.at[f, i])

        def body(d, _):
            cols = pl.ds(pl.multiple_of(d * nport, nport), nport)
            rows_all[pl.ds(f * allcase, ncase), cols] = nat[f, d]
            for q in range(1, nq):
                rows_all[pl.ds(f * allcase + q * ncase, ncase), cols] = gath[f, q, d]
            return 0

        lax.fori_loop(0, pd, body, 0, unroll=4)

    def start_gram(s, value):
        sent, got = gram_refs[s]
        folded = jnp.concatenate(
            [value[8 * r:8 * r + 8] for r in range(value.shape[0] // 8)], axis=1
        )
        sent[...] = folded
        got[0] = folded
        send_parts(lambda i: sent, lambda i: got.at[i], 1 + s, 1)

    def finish_gram(s):
        got = gram_refs[s][1]
        wait_on(got.at[rest], part_rsem.at[1 + s])
        total = jnp.sum(got[...], axis=0)
        return jnp.concatenate(
            [total[:, allcase * r:allcase * (r + 1)] for r in range(total.shape[1] // allcase)],
            axis=0,
        )

    def sym(g):
        return 0.5 * (g + g.T)

    def part(x, j):
        return x[j * width:(j + 1) * width]

    loads = jnp.concatenate([bload_ref[:, k, :] for k in range(ncase)], axis=1)
    lifted = apply_tables(inv_tab, loads)
    inv_keep[...] = lifted
    condensed = -apply_tables(coup_tab, lifted)
    leaving = tall(condensed[pd:])
    for j in range(chunks):
        start_far(0, j, slot_pick, part(leaving, j), 1)
    red_t = [exact(binv_ref[t], coup_ref[t], TN) for t in range(kinds)]
    schur = [pblock_ref[t] - exact(red_t[t], coup_ref[t], TN) for t in range(kinds)]
    schur_tab = split(jnp.concatenate(schur, axis=1))
    red_tab = split(jnp.concatenate(red_t, axis=1))
    own = jnp.concatenate([pload_ref[:, k, :] for k in range(ncase)], axis=0)
    own = own + pick(tall(condensed[:pd]), near_out)
    wait_on(ask_recv.at[rest], part_rsem.at[0])
    port_lane = lax.broadcasted_iota(jnp.int32, (slots, nport), 1).astype(F32)
    asked_pick = jnp.where(ask_recv[...].reshape(slots, nport) == port_lane, 1.0, 0.0).astype(BF16)

    def arrive(e, own, onward):
        pieces = []
        for j in range(chunks):
            piece = part(own, j) + finish_far(e, j, asked_pick)
            if onward:
                start_far(e + 1, j, asked_pick, piece, -1)
            pieces.append(piece)
        return jnp.concatenate(pieces, axis=0)

    def operate(e, near):
        cuts = [0, ((chunks - 1) * width) // pd, ncase] if chunks > 1 else [0, ncase]
        far, near_y, far_y, sent, have = None, None, None, 0, 0
        for a, b in zip(cuts[:-1], cuts[1:]):
            while have * width < b * pd:
                piece = finish_far(e, have, slot_pick)
                far = piece if far is None else jnp.concatenate([far, piece], axis=0)
                have += 1
            rows = slice(a * pd, b * pd)
            ends = jnp.concatenate([wide(near[rows], pd), wide(far[rows], pd)], axis=0)
            y = apply_tables(schur_tab, ends) * stiff[:, a * ncomp:b * ncomp]
            out = tall(y[pd:])
            far_y = out if far_y is None else jnp.concatenate([far_y, out], axis=0)
            out = tall(y[:pd])
            near_y = out if near_y is None else jnp.concatenate([near_y, out], axis=0)
            while (sent + 1) * width <= b * pd:
                start_far(e + 1, sent, slot_pick, part(far_y, sent), 1)
                sent += 1
        return far, pick(near_y, near_out)

    base = arrive(0, own, True)
    publish(0, base)
    far_base, own = operate(1, pick(base, near_in))
    publish(3, far_base)
    forward(0)
    first = arrive(2, own, True)
    publish(1, first)
    near = pick(first, near_in)
    forward(3)
    collect(0)
    far_first, own = operate(3, near)
    forward(1)
    publish(4, far_first)
    collect(1)
    pair = rows_all[0:2 * allcase, :]
    square = exact(pair, pair, NT)
    start_gram(0, jnp.concatenate([square[0:allcase, 0:allcase], square[0:allcase, allcase:], square[allcase:, allcase:]], axis=0))
    second = arrive(4, own, False)
    publish(2, second)
    forward(4)
    collect(3)

    n = allcase
    grams = finish_gram(0)
    g00 = sym(grams[0:n])
    g01 = sym(grams[n:2 * n])
    g11 = sym(grams[2 * n:3 * n])
    step1 = gauss_solve(g01, g00)
    forward(2)
    cross = exact(g01, step1)
    g1 = sym(g00 - cross - cross.T + exact(step1, exact(g11, step1), TN))
    turn = gauss_solve(g00, g1)
    eye = jnp.where(
        lax.broadcasted_iota(jnp.int32, (n, n), 0) == lax.broadcasted_iota(jnp.int32, (n, n), 1),
        1.0,
        0.0,
    )
    lead = turn + eye
    mixed = exact(lead, exact(g11, step1), TN)
    known = exact(lead, exact(g01, lead), TN) - mixed - mixed.T

    collect(4)
    collect(2)
    start_gram(1, exact(rows_all[n:2 * n, :], rows_all[2 * n:3 * n, :], NT))
    g12 = sym(finish_gram(1))
    curve = sym(known + exact(step1, exact(g12, step1), TN))
    step2 = gauss_solve(curve, g1)
    alpha = step1 + exact(lead, step2)
    beta = exact(step1, step2)
    at = alpha.T[0:ncase]
    bt = beta.T[0:ncase]
    zero = jnp.zeros_like(at)
    coefs = jnp.concatenate(
        [
            jnp.concatenate([at, -bt, zero], axis=1),
            jnp.concatenate([zero, -at, bt], axis=1),
        ],
        axis=0,
    )
    ctop, clow = split(coefs)
    both = jnp.concatenate([ctop, clow], axis=0)
    vtop, vlow = split(rows_all[0:3 * allcase, :])
    part_a = mm(both, vtop)
    mixed_rows = part_a[0:2 * ncase] + part_a[2 * ncase:] + mm(ctop, vlow)
    for d in range(pd):
        cols = slice(d * nport, (d + 1) * nport)
        sol_ref[d] = mixed_rows[0:ncase, cols]
        res_ref[d] = nat[0, d] + mixed_rows[ncase:, cols]

    answer = jnp.concatenate([sol_ref[:, k, :] for k in range(ncase)], axis=0)
    ftop, flow = split(rows_all[3 * allcase:, :])
    lead_a = jnp.concatenate([ctop[0:ncase, 0:2 * n], clow[0:ncase, 0:2 * n]], axis=0)
    part_f = mm(lead_a, ftop)
    far_rows = part_f[0:ncase] + part_f[ncase:] + mm(ctop[0:ncase, 0:2 * n], flow)
    for d in range(pd):
        nat_far[d] = far_rows[:, d * nport:(d + 1) * nport]
    near = wide(pick(answer, near_in), pd)
    ends = jnp.concatenate(
        [near, jnp.concatenate([nat_far[:, k, :] for k in range(ncase)], axis=1)], axis=0
    )
    scaled = inv_keep[...] / stiff
    back = scaled - apply_tables(red_tab, ends)
    for k in range(ncase):
        bub_ref[:, k, :] = back[:, k * ncomp:(k + 1) * ncomp]

    wait_on(ask_send.at[rest], part_ssem.at[0])
    for e in range(5):
        for j in range(chunks):
            wait_on(far_send.at[e, j, rest], part_ssem.at[3 + e * chunks + j])
    for s in range(2):
        wait_on(gram_refs[s][1].at[rest], part_ssem.at[1 + s])
    for f in range(5):
        for i in range(1, nq):
            wait_on(nat.at[f], case_ssem.at[f, i])


def local(
    comp_type,
    stiffness,
    near_port,
    far_owner,
    far_port,
    bubble_load,
    port_load,
    bubble_inverse,
    coupling,
    port_block,
):
    npy = lax.axis_size("py")
    parts = lax.axis_size("px") * npy
    nq = lax.axis_size("case")
    ncomp = comp_type.shape[0]
    modes, ncase, _ = bubble_load.shape
    pd, _, nport = port_load.shape
    cap = 3 * ncomp // (2 * parts)
    depth = -(-cap // 8) * 8
    allcase = nq * ncase
    width = 128 if (ncase * pd) % 128 == 0 else ncase * pd
    chunks = ncase * pd // width
    idx = jnp.stack([comp_type, near_port, far_owner[:, 0], far_port])
    vmem = pl.BlockSpec(memory_space=pltpu.VMEM)

    def body(*refs):
        kernel((parts, npy, nq, depth, width, chunks), *refs)

    return pl.pallas_call(
        body,
        out_shape=(
            jax.ShapeDtypeStruct(port_load.shape, F32),
            jax.ShapeDtypeStruct(port_load.shape, F32),
            jax.ShapeDtypeStruct(bubble_load.shape, F32),
        ),
        in_specs=[vmem] * 7,
        out_specs=(vmem, vmem, vmem),
        scratch_shapes=[
            pltpu.VMEM((parts, depth, nport), F32),
            pltpu.VMEM((parts, depth, nport), F32),
            pltpu.VMEM((5, chunks, parts, depth, width), F32),
            pltpu.VMEM((5, chunks, parts, depth, width), F32),
            pltpu.VMEM((5, pd, ncase, nport), F32),
            pltpu.VMEM((5, nq, pd, ncase, nport), F32),
            pltpu.VMEM((5 * allcase, pd * nport), F32),
            pltpu.VMEM((8, 3 * allcase * allcase // 8), F32),
            pltpu.VMEM((parts, 8, 3 * allcase * allcase // 8), F32),
            pltpu.VMEM((8, allcase * allcase // 8), F32),
            pltpu.VMEM((parts, 8, allcase * allcase // 8), F32),
            pltpu.VMEM((modes, ncase * ncomp), F32),
            pltpu.VMEM((pd, ncase, nport), F32),
            pltpu.SemaphoreType.DMA((3 + 5 * chunks,)),
            pltpu.SemaphoreType.DMA((3 + 5 * chunks,)),
            pltpu.SemaphoreType.DMA((5, nq)),
            pltpu.SemaphoreType.DMA((5, nq)),
        ],
        compiler_params=pltpu.CompilerParams(
            collective_id=0, has_side_effects=True, vmem_limit_bytes=60 * 1024 * 1024
        ),
        name="condensed_solve",
    )(
        idx,
        stiffness.reshape(1, ncomp),
        bubble_load,
        port_load,
        bubble_inverse,
        jnp.swapaxes(coupling, 1, 2),
        port_block,
    )


def solution(mesh):
    placed = (
        P(("px", "py")),
        P(("px", "py")),
        P(("px", "py")),
        P(("px", "py"), None),
        P(("px", "py")),
        P(None, "case", ("px", "py")),
        P(None, "case", ("px", "py")),
        P(),
        P(),
        P(),
    )
    return jax.shard_map(
        local,
        mesh=mesh,
        in_specs=placed,
        out_specs=(
            P(None, "case", ("px", "py")),
            P(None, "case", ("px", "py")),
            P(None, "case", ("px", "py")),
        ),
        check_vma=False,
    )
```
